32 devices in a mesh: dp: 8 (over z, y), section: 4 (over x, core).
Axes of the slice: x: 2, y: 2, z: 4, core: 2. Of those that a mesh axis runs over, the one named last changes fastest.
Arguments:
- section_inputs: bfloat16 [4, 4096, 1536], P('section', 'dp'), may hold values from -6 to 6
- top_grad: bfloat16 [4096, 1536], P('dp'), may hold values from -6 to 6
- proj_weight: bfloat16 [4, 1536, 1536], P('section'), may hold values from -0.15625 to 0.15625
- norm_gain: float32 [4, 1536], P('section'), may hold values from 0.25 to 1.75
- dw_kernel: float32 [4, 32, 1536], P('section'), may hold values from -1 to 1
- tile_frames: int32 [32], P('dp'), may hold values from 0 to 128, as said below
Outputs:
- input_grads: bfloat16 [4, 4096, 1536], P('section', 'dp')
- weight_grads: float32 [4, 1536, 1536], P('section', 'dp')
- kernel_grads: float32 [4, 32, 1536], P('section')
- gain_grads: float32 [4, 1536], P('section')
The draws below stay inside these ranges and needn't reach their ends.
Inputs may be any that keep to these rules, and one draw needn't show every extreme that they name: `tile_frames`: in each group of 4 consecutive slots (the slots of one index of dp) the non-empty slots come first, the first slot holds 128 frames, and non-empty slots hold 32 to 128 frames; in some group all 4 slots are non-empty.
All inputs are finite; a program needn't handle non-finite values.
Results may differ from the reference program's by a relative error of at most 0.01.
Values may be sent and summed in bfloat16 or wider, within the bound.
A program may use at most 128 MiB of HBM per device.

```python
import jax
import jax.numpy as jnp
from jax import lax

D = 1536
K = 32
TILE = 128
SLOTS = 4
SECTIONS = 4
TILES = 32
TOKENS = 4096


def draw_tile_frames(key, part):
    groups = TILES // SLOTS
    key_live, key_frames, key_full = jax.random.split(jax.random.fold_in(key, 7), 3)
    live_count = jax.random.randint(key_live, (groups,), 1, SLOTS + 1)
    full_group = jax.random.randint(key_full, (), 0, groups)
    live_count = jnp.where(jnp.arange(groups) == full_group, SLOTS, live_count)
    frames = jax.random.randint(key_frames, (groups, SLOTS), TILE // 4, TILE + 1)
    slot_ids = jnp.arange(SLOTS)[None, :]
    frames = jnp.where(slot_ids == 0, TILE, frames)
    frames = jnp.where(slot_ids < live_count[:, None], frames, 0)
    return frames.reshape(-1).astype(jnp.int32)


def spiked(entries, key, source, target, blocks, factor):
    owner, partner = [(jnp.arange(entries.shape[dim]) // (entries.shape[dim] // blocks)).reshape([-1 if axis == dim else 1 for axis in range(entries.ndim)]) for dim in (source, target)]
    chosen = jax.random.permutation(key, blocks)[partner]
    strong = (owner == chosen) | (owner == (partner + blocks // 2) % blocks)
    return jnp.where(strong, factor * entries, entries)


def level_of(key, extent, cuts, low, top_value):
    loudness = 1.0
    for position, blocks in cuts:
        heights = jax.random.uniform(jax.random.fold_in(jax.random.fold_in(key, 6), position), (blocks,), jnp.float32, low / len(cuts), top_value / len(cuts))
        loudness = loudness * jnp.repeat(jnp.exp(heights), extent[position] // blocks).reshape((-1,) + (1,) * (len(extent) - 1 - position))
    return loudness


def bell_draw(rng, extent, deviation, limit, shards=(), dtype=jnp.bfloat16):
    factor_of = level_of(rng, extent, shards, -0.22, 0.18) if shards else 1.0
    entries = jax.random.normal(rng, extent, jnp.float32) * deviation * factor_of
    return jnp.minimum(jnp.maximum(entries, -limit), limit).astype(dtype)


def noise_with(key, dims, scale, limit, cuts, heavy, kind=jnp.bfloat16):
    drawn = scale * jax.random.normal(key, dims, jnp.float32)
    if cuts:
        drawn = drawn * level_of(key, dims, cuts, -0.22, 0.18)
    return jnp.clip(spiked(drawn, jax.random.fold_in(key, 3), *heavy), -limit, limit).astype(kind)


def setup_inputs(seed: int = 0) -> dict:
    key_list = jax.random.split(jax.random.key(seed), 7)
    return {
        "section_inputs": noise_with(key_list[0], (SECTIONS, TOKENS, D), 1.0, 6.0, ((0, 4), (1, 8)), (1, 2, 8, 2.0)),
        "top_grad": bell_draw(key_list[1], (TOKENS, D), 1.0, 6.0, ((0, 8),)),
        "proj_weight": bell_draw(key_list[2], (SECTIONS, D, D), D ** -0.5, 0.15625, ((0, 4),)),
        "norm_gain": jnp.clip(1.0 + 0.15 * jax.random.normal(key_list[3], (SECTIONS, D), jnp.float32), 0.25, 1.75),
        "dw_kernel": bell_draw(key_list[4], (SECTIONS, K, D), K ** -0.5, 1.0, ((0, 4),), jnp.float32),
        "tile_frames": draw_tile_frames(jax.random.fold_in(key_list[6], 71), 0),
    }


def section_parts(inputs, gain_row, kernel, frame_mask):
    centre = inputs - lax.optimization_barrier(jnp.mean(inputs, axis=-1, keepdims=True))
    spread = lax.optimization_barrier(jnp.mean(centre * centre, axis=-1, keepdims=True))
    normed = centre * lax.rsqrt(spread + 1e-05) * gain_row
    masked = normed * frame_mask
    length = inputs.shape[1]
    tap_count = kernel.shape[0]
    before = tap_count // 2
    padded = jnp.pad(masked, ((0, 0), (before, tap_count - 1 - before), (0, 0)))
    conved = jnp.zeros_like(masked)
    for offset in range(tap_count):
        conved = conved + kernel[offset] * padded[:, offset:offset + length, :]
    return (conved * jax.nn.sigmoid(conved)).astype(jnp.bfloat16)

def section_backward(inputs, cotangent, weight, gain_row, kernel, frame_mask):

    def local_part(values, gain_vals, kernel_taps):
        return section_parts(values, gain_vals, kernel_taps, frame_mask)
    hidden, backward = jax.vjp(local_part, inputs.astype(jnp.float32), gain_row, kernel)
    flat_hidden = hidden.reshape(cotangent.shape)
    hidden_grad = lax.dot_general(cotangent, weight, (((1,), (1,)), ((), ())), preferred_element_type=jnp.float32).astype(jnp.bfloat16)
    input_part, gain_part, kernel_part = backward(hidden_grad.reshape(hidden.shape))
    input_grad = (cotangent.astype(jnp.float32) + input_part.reshape(cotangent.shape)).astype(jnp.bfloat16)
    return (input_grad, flat_hidden, gain_part, kernel_part)

def reference(section_inputs, top_grad, proj_weight, norm_gain, dw_kernel, tile_frames):
    block_count = TILES // SLOTS
    block_rows = SLOTS * TILE
    inputs_blocks = jnp.moveaxis(section_inputs.reshape(SECTIONS, block_count, SLOTS, TILE, D), 1, 0)
    top_blocks = top_grad.reshape(block_count, block_rows, D)
    frame_blocks = tile_frames.reshape(block_count, SLOTS)

    def one_block(carry, pieces):
        weight_acc, gain_acc, kernel_acc = carry
        inputs_all, top_piece, frames = pieces
        frame_mask = (jnp.arange(TILE)[None, :] < frames[:, None]).astype(jnp.float32)[:, :, None]
        cotangent = (top_piece.astype(jnp.float32) * frame_mask.reshape(block_rows, 1)).astype(jnp.bfloat16)
        grads_list = [None] * SECTIONS
        for section_id in reversed(range(SECTIONS)):
            input_grad, flat_hidden, gain_part, kernel_part = section_backward(inputs_all[section_id], cotangent, proj_weight[section_id], norm_gain[section_id], dw_kernel[section_id], frame_mask)
            weight_term = lax.dot_general(flat_hidden, cotangent, (((0,), (0,)), ((), ())), preferred_element_type=jnp.float32)
            weight_acc = weight_acc.at[section_id].add(weight_term)
            gain_acc = gain_acc.at[section_id].add(gain_part)
            kernel_acc = kernel_acc.at[section_id].add(kernel_part)
            grads_list[section_id] = input_grad
            cotangent = input_grad
        return ((weight_acc, gain_acc, kernel_acc), jnp.stack(grads_list))
    init = (jnp.zeros((SECTIONS, D, D), jnp.float32), jnp.zeros((SECTIONS, D), jnp.float32), jnp.zeros((SECTIONS, K, D), jnp.float32))
    totals, grads_blocks = lax.scan(one_block, init, (inputs_blocks, top_blocks, frame_blocks))
    weight_acc, gain_acc, kernel_acc = totals
    input_grads = jnp.moveaxis(grads_blocks, 1, 0).reshape(SECTIONS, TOKENS, D)
    return (input_grads, weight_acc, kernel_acc, gain_acc)
```

```python
import functools

import jax
import jax.numpy as jnp
from jax import lax
from jax.experimental import pallas as pl
from jax.experimental.pallas import tpu as pltpu
from jax.sharding import PartitionSpec as P

TILE = 128
MESH = pl.DeviceIdType.MESH


def exchange_kernel(n, big_ref, small_ref, big_out, small_out, big_held, small_held, sems):
    me = lax.axis_index("dp")
    barrier = pltpu.get_barrier_semaphore()
    for step in range(1, n):
        peer = lax.rem(me + step, n)
        pl.semaphore_signal(barrier, inc=1, device_id={"dp": peer}, device_id_type=MESH)
    pl.semaphore_wait(barrier, n - 1)
    copies = []
    for step in range(1, n):
        peer = lax.rem(me + step, n)
        pair = []
        for kind, (src, dst) in enumerate(
            ((small_ref, small_held.at[step]), (big_ref.at[peer], big_held.at[step]))
        ):
            copy = pltpu.make_async_remote_copy(
                src_ref=src,
                dst_ref=dst,
                send_sem=sems.at[kind, 0, step],
                recv_sem=sems.at[kind, 1, step],
                device_id={"dp": peer},
                device_id_type=MESH,
            )
            copy.start()
            pair.append(copy)
        copies.append(pair)
    small_out[...] = small_ref[...].astype(jnp.float32)
    big_out[...] = big_ref[me].astype(jnp.float32)
    for step in range(1, n):
        small_copy, big_copy = copies[step - 1]
        small_copy.wait()
        small_out[...] += small_held[step].astype(jnp.float32)
        big_copy.wait()
        big_out[...] += big_held[step].astype(jnp.float32)


def sum_over_dp(big, small):
    n, rows, width = big.shape
    return pl.pallas_call(
        functools.partial(exchange_kernel, n),
        out_shape=(
            jax.ShapeDtypeStruct((rows, width), jnp.float32),
            jax.ShapeDtypeStruct(small.shape, jnp.float32),
        ),
        in_specs=[pl.BlockSpec(memory_space=pltpu.VMEM)] * 2,
        out_specs=(pl.BlockSpec(memory_space=pltpu.VMEM),) * 2,
        scratch_shapes=[
            pltpu.VMEM((n, rows, width), jnp.bfloat16),
            pltpu.VMEM((n,) + small.shape, jnp.bfloat16),
            pltpu.SemaphoreType.DMA((2, 2, n)),
        ],
        compiler_params=pltpu.CompilerParams(
            collective_id=0, has_side_effects=True, vmem_limit_bytes=48 * 1024 * 1024
        ),
    )(big, small)


def shards(section_inputs, top_grad, proj_weight, norm_gain, dw_kernel, tile_frames):
    dp_count = lax.axis_size("dp")
    section_count = lax.axis_size("section")
    section_index = lax.axis_index("section")
    slots = tile_frames.shape[0]
    width = proj_weight.shape[-1]
    taps = dw_kernel.shape[1]
    before = taps // 2
    x = section_inputs[0].reshape(slots, TILE, width).astype(jnp.float32)
    weight = proj_weight[0]
    gain = norm_gain[0]
    kernel = dw_kernel[0]
    mask = (jnp.arange(TILE)[None, :] < tile_frames[:, None]).astype(jnp.float32)[:, :, None]

    centre = x - jnp.mean(x, axis=-1, keepdims=True)
    rstd = lax.rsqrt(jnp.mean(centre * centre, axis=-1, keepdims=True) + 1e-05)
    normed = centre * rstd
    padded = jnp.pad(normed * gain * mask, ((0, 0), (before, taps - 1 - before), (0, 0)))
    conv = kernel[0] * padded[:, 0:TILE]
    for k in range(1, taps):
        conv = conv + kernel[k] * padded[:, k : k + TILE]
    sig = jax.nn.sigmoid(conv)
    hidden = (conv * sig).astype(jnp.bfloat16)
    slope = sig * (1.0 + conv * (1.0 - sig))
    top = (top_grad.reshape(slots, TILE, width).astype(jnp.float32) * mask).astype(jnp.bfloat16)

    ticks = slots + section_count - 1
    lag = section_count - 1 - section_index
    is_last = section_index == section_count - 1
    cots, dconvs, dmaskeds, grads = [], [], [], []
    incoming = jnp.zeros((TILE, width), jnp.bfloat16)
    for tick in range(ticks):
        slot = jnp.clip(tick - lag, 0, slots - 1)
        pick = lambda a: lax.dynamic_index_in_dim(a, slot, 0, keepdims=False)
        cot = jnp.where(is_last, top[min(tick, slots - 1)], incoming)
        hidden_grad = lax.dot_general(
            cot, weight, (((1,), (1,)), ((), ())), preferred_element_type=jnp.float32
        ).astype(jnp.bfloat16)
        dconv = hidden_grad.astype(jnp.float32) * pick(slope)
        dpad = jnp.pad(dconv, ((taps - 1 - before, before), (0, 0)))
        dmasked = kernel[taps - 1] * dpad[0:TILE]
        for o in range(1, taps):
            dmasked = dmasked + kernel[taps - 1 - o] * dpad[o : o + TILE]
        dmasked = dmasked * pick(mask)
        unit = pick(normed)
        g = dmasked * gain
        part = pick(rstd) * (
            g
            - jnp.mean(g, axis=-1, keepdims=True)
            - unit * jnp.mean(g * unit, axis=-1, keepdims=True)
        )
        grad = (cot.astype(jnp.float32) + part).astype(jnp.bfloat16)
        cots.append(cot)
        dconvs.append(dconv)
        dmaskeds.append(dmasked)
        grads.append(grad)
        pairs = [
            (s, s - 1)
            for s in range(1, section_count)
            if 0 <= tick - (section_count - 1 - s) < slots
        ]
        if pairs:
            incoming = lax.ppermute(grad, "section", pairs)

    own = lambda parts: lax.dynamic_slice_in_dim(jnp.stack(parts), lag, slots, 0)
    input_grads = own(grads).reshape(slots * TILE, width)
    cot_all = own(cots).reshape(slots * TILE, width)
    weight_part = lax.dot_general(
        hidden.reshape(slots * TILE, width),
        cot_all,
        (((0,), (0,)), ((), ())),
        preferred_element_type=jnp.float32,
    ).astype(jnp.bfloat16)
    dconv_all = own(dconvs)
    gain_part = jnp.sum(own(dmaskeds) * normed, axis=(0, 1))
    kernel_part = [
        jnp.sum(dconv_all * padded[:, k : k + TILE], axis=(0, 1)) for k in range(taps)
    ]
    fill = -(taps + 1) % 16
    small = jnp.stack(kernel_part + [gain_part] + [jnp.zeros_like(gain_part)] * fill)
    big_sum, small_sum = sum_over_dp(
        weight_part.reshape(dp_count, width // dp_count, width), small.astype(jnp.bfloat16)
    )
    return (input_grads[None], big_sum[None], small_sum[None, :taps], small_sum[None, taps])


def solution(mesh):
    in_specs = (
        P("section", "dp", None),
        P("dp", None),
        P("section", None, None),
        P("section", None),
        P("section", None, None),
        P("dp"),
    )
    out_specs = (
        P("section", "dp", None),
        P("section", "dp", None),
        P("section", None, None),
        P("section", None),
    )
    return jax.shard_map(shards, mesh=mesh, in_specs=in_specs, out_specs=out_specs, check_vma=False)
```

```python
import functools

import jax
import jax.numpy as jnp
from jax import lax
from jax.experimental import pallas as pl
from jax.experimental.pallas import tpu as pltpu
from jax.sharding import PartitionSpec as P

TILE = 128
MESH = pl.DeviceIdType.MESH


def exchange_kernel(
    n,
    big_ref,
    small_ref,
    big_out,
    small_out,
    near_big,
    near_small,
    send_big,
    send_small,
    far_big,
    far_small,
    near_sems,
    far_sems,
):
    pairs = n // 2
    me = lax.axis_index("dp")
    side, pair = lax.rem(me, 2), lax.div(me, 2)
    partner = pair * 2 + 1 - side
    order = list(range(1, pairs)) + [0]
    owner = lambda step: lax.rem(pair + step, pairs)

    barrier = pltpu.get_barrier_semaphore()
    pl.semaphore_signal(barrier, inc=1, device_id={"dp": partner}, device_id_type=MESH)
    for step in range(1, pairs):
        peer = owner(step) * 2 + side
        pl.semaphore_signal(barrier, inc=1, device_id={"dp": peer}, device_id_type=MESH)
    pl.semaphore_wait(barrier, pairs)

    def send(src, dst, sems, index, device):
        copy = pltpu.make_async_remote_copy(
            src_ref=src,
            dst_ref=dst,
            send_sem=sems.at[0, index],
            recv_sem=sems.at[1, index],
            device_id={"dp": device},
            device_id_type=MESH,
        )
        copy.start()
        return copy

    small_near = send(small_ref, near_small, near_sems, pairs, partner)
    near = {
        step: send(
            big_ref.at[owner(step) * 2 + 1 - side], near_big.at[step], near_sems, step, partner
        )
        for step in order
    }
    far = {}
    small_near.wait()
    send_small[...] = (
        small_ref[...].astype(jnp.float32) + near_small[...].astype(jnp.float32)
    ).astype(jnp.bfloat16)
    small_out[...] = send_small[...].astype(jnp.float32)
    small_far = {
        step: send(
            send_small, far_small.at[step], far_sems, pairs + step, owner(step) * 2 + side
        )
        for step in order[:-1]
    }
    for step in order[:-1]:
        near[step].wait()
        send_big[step] = (
            big_ref[owner(step) * 2 + side].astype(jnp.float32)
            + near_big[step].astype(jnp.float32)
        ).astype(jnp.bfloat16)
        far[step] = send(
            send_big.at[step], far_big.at[step], far_sems, step, owner(step) * 2 + side
        )
    near[0].wait()
    big_out[...] = big_ref[me].astype(jnp.float32) + near_big[0].astype(jnp.float32)
    for step in order[:-1]:
        small_far[step].wait()
        small_out[...] += far_small[step].astype(jnp.float32)
        far[step].wait()
        big_out[...] += far_big[step].astype(jnp.float32)


def sum_over_dp(big, small):
    n, rows, width = big.shape
    pairs = n // 2
    blocks = pltpu.VMEM((pairs, rows, width), jnp.bfloat16)
    return pl.pallas_call(
        functools.partial(exchange_kernel, n),
        out_shape=(
            jax.ShapeDtypeStruct((rows, width), jnp.float32),
            jax.ShapeDtypeStruct(small.shape, jnp.float32),
        ),
        in_specs=[pl.BlockSpec(memory_space=pltpu.VMEM)] * 2,
        out_specs=(pl.BlockSpec(memory_space=pltpu.VMEM),) * 2,
        scratch_shapes=[
            blocks,
            pltpu.VMEM(small.shape, jnp.bfloat16),
            blocks,
            pltpu.VMEM(small.shape, jnp.bfloat16),
            blocks,
            pltpu.VMEM((pairs,) + small.shape, jnp.bfloat16),
            pltpu.SemaphoreType.DMA((2, pairs + 1)),
            pltpu.SemaphoreType.DMA((2, 2 * pairs)),
        ],
        compiler_params=pltpu.CompilerParams(
            collective_id=0, has_side_effects=True, vmem_limit_bytes=48 * 1024 * 1024
        ),
    )(big, small)


def taps_kernel(taps, slot_ref, dconv_ref, padded_ref, after_ref, out_ref):
    for k in range(taps):
        out_ref[k : k + 1, :] = jnp.sum(
            dconv_ref[...] * padded_ref[0, k : k + TILE, :], axis=0, keepdims=True
        )


def kernel_grad(slot, dconv, padded, after, taps):
    width = dconv.shape[-1]
    lanes = 128
    return pl.pallas_call(
        functools.partial(taps_kernel, taps),
        grid_spec=pltpu.PrefetchScalarGridSpec(
            num_scalar_prefetch=1,
            grid=(width // lanes,),
            in_specs=[
                pl.BlockSpec((TILE, lanes), lambda j, s: (0, j)),
                pl.BlockSpec((1, padded.shape[1], lanes), lambda j, s: (s[0], 0, j)),
                pl.BlockSpec(memory_space=pl.ANY),
            ],
            out_specs=pl.BlockSpec((taps, lanes), lambda j, s: (0, j)),
        ),
        out_shape=jax.ShapeDtypeStruct((taps, width), jnp.float32),
        cost_estimate=pl.CostEstimate(
            flops=2 * taps * TILE * width, bytes_accessed=8 * TILE * width, transcendentals=0
        ),
        compiler_params=pltpu.CompilerParams(vmem_limit_bytes=8 * 1024 * 1024),
    )(slot.reshape(1), dconv, padded, after)


def shards(section_inputs, top_grad, proj_weight, norm_gain, dw_kernel, tile_frames):
    dp_count = lax.axis_size("dp")
    section_count = lax.axis_size("section")
    section_index = lax.axis_index("section")
    slots = tile_frames.shape[0]
    width = proj_weight.shape[-1]
    taps = dw_kernel.shape[1]
    before = taps // 2
    x = section_inputs[0].reshape(slots, TILE, width).astype(jnp.float32)
    weight = proj_weight[0]
    gain = norm_gain[0]
    kernel = dw_kernel[0]
    mask = (jnp.arange(TILE)[None, :] < tile_frames[:, None]).astype(jnp.float32)[:, :, None]

    centre = x - jnp.mean(x, axis=-1, keepdims=True)
    rstd = lax.rsqrt(jnp.mean(centre * centre, axis=-1, keepdims=True) + 1e-05)
    normed = centre * rstd
    padded = jnp.pad(normed * gain * mask, ((0, 0), (before, taps - before), (0, 0)))
    conv = kernel[0] * padded[:, 0:TILE]
    for k in range(1, taps):
        conv = conv + kernel[k] * padded[:, k : k + TILE]
    sig = jax.nn.sigmoid(conv)
    hidden = (conv * sig).astype(jnp.bfloat16)
    slope = sig * (1.0 + conv * (1.0 - sig))
    top = (top_grad.reshape(slots, TILE, width).astype(jnp.float32) * mask).astype(jnp.bfloat16)

    ticks = slots + section_count - 1
    lag = section_count - 1 - section_index
    is_last = section_index == section_count - 1
    cots, grads = [], []
    gain_part = jnp.zeros_like(gain)
    kernel_part = jnp.zeros_like(kernel)
    incoming = jnp.zeros((TILE, width), jnp.bfloat16)
    for tick in range(ticks):
        slot = jnp.clip(tick - lag, 0, slots - 1)
        pick = lambda a: lax.dynamic_index_in_dim(a, slot, 0, keepdims=False)
        cot = jnp.where(is_last, top[min(tick, slots - 1)], incoming)
        hidden_grad = lax.dot_general(
            cot, weight, (((1,), (1,)), ((), ())), preferred_element_type=jnp.float32
        ).astype(jnp.bfloat16)
        dconv = hidden_grad.astype(jnp.float32) * pick(slope)
        dpad = jnp.pad(dconv, ((taps - 1 - before, before), (0, 0)))
        dmasked = kernel[taps - 1] * dpad[0:TILE]
        for o in range(1, taps):
            dmasked = dmasked + kernel[taps - 1 - o] * dpad[o : o + TILE]
        dmasked = dmasked * pick(mask)
        unit = pick(normed)
        g = dmasked * gain
        part = pick(rstd) * (
            g
            - jnp.mean(g, axis=-1, keepdims=True)
            - unit * jnp.mean(g * unit, axis=-1, keepdims=True)
        )
        grad = (cot.astype(jnp.float32) + part).astype(jnp.bfloat16)
        cots.append(cot)
        grads.append(grad)
        pairs = [
            (s, s - 1)
            for s in range(1, section_count)
            if 0 <= tick - (section_count - 1 - s) < slots
        ]
        if pairs:
            incoming = lax.ppermute(grad, "section", pairs)
        active = jnp.logical_and(tick >= lag, tick < lag + slots)
        gain_part += jnp.where(active, jnp.sum(dmasked * unit, axis=0), 0.0)
        kernel_part += jnp.where(
            active, kernel_grad(slot.astype(jnp.int32), dconv, padded, grad, taps), 0.0
        )
        incoming, kernel_part = lax.optimization_barrier((incoming, kernel_part))

    own = lambda parts: lax.dynamic_slice_in_dim(jnp.stack(parts), lag, slots, 0)
    input_grads = own(grads).reshape(slots * TILE, width)
    cot_all = own(cots).reshape(slots * TILE, width)
    weight_part = lax.dot_general(
        hidden.reshape(slots * TILE, width),
        cot_all,
        (((0,), (0,)), ((), ())),
        preferred_element_type=jnp.float32,
    ).astype(jnp.bfloat16)
    fill = -(taps + 1) % 16
    small = jnp.concatenate([kernel_part, gain_part[None], jnp.zeros((fill, width))])
    big_sum, small_sum = sum_over_dp(
        weight_part.reshape(dp_count, width // dp_count, width), small.astype(jnp.bfloat16)
    )
    return (input_grads[None], big_sum[None], small_sum[None, :taps], small_sum[None, taps])


def solution(mesh):
    in_specs = (
        P("section", "dp", None),
        P("dp", None),
        P("section", None, None),
        P("section", None),
        P("section", None, None),
        P("dp"),
    )
    out_specs = (
        P("section", "dp", None),
        P("section", "dp", None),
        P("section", None, None),
        P("section", None),
    )
    return jax.shard_map(shards, mesh=mesh, in_specs=in_specs, out_specs=out_specs, check_vma=False)
```
